32 devices in a mesh: rep: 4 (over y, core), tp: 8 (over z, x).
Axes of the slice: x: 2, y: 2, z: 4, core: 2. Of those that a mesh axis runs over, the one named last changes fastest.
Arguments:
- tokens: bfloat16 [2560, 5120], P(('rep', 'tp')), parts along dimension 0
- weights: bfloat16 [3, 5120, 4096], P(None, None, 'tp')
- modulation: float32 [2, 36, 5120], P(None, 'rep'), parts along dimension 1, may hold values from -3 to 3
- qk_gain: float32 [2, 4096], P(None, 'tp'), may hold values from 0.25 to 1.75
- segment_ids: int32 [2560], P('rep'), parts along dimension 0, may hold values from 0 to 9, as said below
- positions: int32 [3, 2560], P(None, 'rep'), parts along dimension 1, may hold values from 0 to 15, as said below
- page_table: int32 [160], P('rep'), parts along dimension 0, may hold values from 0 to 79, as said below
- kv_cache: bfloat16 [2, 32, 320, 16, 128], P(None, 'tp', 'rep'), parts along dimension 2, may hold values from -6 to 6
Outputs:
- attended: bfloat16 [2560, 4096], P(('rep', 'tp')), parts along dimension 0
- new_cache: bfloat16 [2, 32, 320, 16, 128], P(None, 'tp', 'rep'), parts along dimension 2
The draws below stay inside these ranges and needn't reach their ends.
There are 4 independent parts, one for each index of `rep`. The reference program is written for one: setup_inputs(seed, part) draws one part's arguments, and reference() takes and returns one part's arrays. A program takes and returns all parts, laid end to end along the dimension named above; an argument that names none is the same for every part. Nothing has to cross between parts.
Inputs may be any that keep to these rules, and one draw needn't show every extreme that they name: `segment_ids`: never falling; 0 on the first 512 tokens (the long clip); then clips 1 to 8 in order, each of 8 to 16 tokens, at least one of exactly 16; the remaining tokens are padding with id 9. `positions`: each token's frame, height and width index on its clip's grid; 0 on padding tokens. `page_table`: distinct pages.
All inputs are finite; a program needn't handle non-finite values.
Results may differ from the reference program's by a relative error of at most 0.0047.
Values may be sent and summed in bfloat16 or wider, within the bound.
No kernel may reach another device: no remote copies, remote signals or barrier semaphores. Data moves between devices by JAX's collectives and lax.ppermute only.
A program may use at most 128 MiB of HBM per device.

```python
import jax
import jax.numpy as jnp
import numpy as np
from jax import lax

D = 5120
HEAD = 128
HEADS = 32
SHORTS = 8
PAGE = 16
TOKENS = 640
LONG = 512
SLOT = 16
CLIPS = 9
HD = 4096
NPAGES = 40
POOL = 80


def clip_lengths(key):
    keyed = jax.random.fold_in(key, 11)
    lengths = jax.random.randint(jax.random.fold_in(keyed, 1), (SHORTS,), SLOT // 2, SLOT + 1)
    chosen = jax.random.randint(jax.random.fold_in(keyed, 2), (), 0, SHORTS)
    return jnp.where(jnp.arange(SHORTS, dtype=jnp.int32) == chosen, SLOT, lengths).astype(jnp.int32)


def short_clip_index(key):
    lengths = clip_lengths(key)
    ends = jnp.cumsum(lengths).astype(jnp.int32)
    slots = jnp.arange(SHORTS * SLOT, dtype=jnp.int32)
    clip_index = jnp.sum((slots[:, None] >= ends[None, :]).astype(jnp.int32), axis=1)
    return (slots, clip_index, ends - lengths)


def draw_segment_ids(key, part):
    slots, clip_index, starts = short_clip_index(key)
    return jnp.concatenate([jnp.zeros((LONG,), jnp.int32), 1 + clip_index]).astype(jnp.int32)


def draw_positions(key, part):
    slots, clip_index, starts = short_clip_index(key)
    is_live = clip_index < SHORTS
    clip_safe = jnp.minimum(clip_index, SHORTS - 1)
    local_index = slots - starts[clip_safe]
    offsets = jax.random.randint(jax.random.fold_in(key, 12), (SHORTS,), 0, 8)
    frame_short = jnp.where(is_live, offsets[clip_safe], 0)
    height_short = jnp.where(is_live, local_index // 8, 0)
    width_short = jnp.where(is_live, local_index % 8, 0)
    long_index = jnp.arange(LONG, dtype=jnp.int32)
    frame_rows = jnp.concatenate([long_index // 256, frame_short])
    height_rows = jnp.concatenate([long_index // 16 % 16, height_short])
    width_rows = jnp.concatenate([long_index % 16, width_short])
    return jnp.stack([frame_rows, height_rows, width_rows]).astype(jnp.int32)


def draw_page_table(key, part):
    keyed = jax.random.fold_in(key, 13)
    order = jax.random.permutation(jax.random.fold_in(keyed, 1), NPAGES).astype(jnp.int32)
    parity = jax.random.randint(jax.random.fold_in(keyed, 2), (NPAGES,), 0, 2)
    parity = jnp.where(order == NPAGES - 1, 1, parity)
    return (2 * order + parity).astype(jnp.int32)


def log_uniform(key, shape, lower, upper):
    return jnp.exp(jax.random.uniform(key, shape, jnp.float32, jnp.log(lower), jnp.log(upper)))


def draw_tokens(key, part):
    keyed = jax.random.fold_in(key, 1)
    row_scale = log_uniform(jax.random.fold_in(keyed, 2), (TOKENS, 1), 0.3, 4.0)
    col_scale = log_uniform(jax.random.fold_in(keyed, 3), (1, D), 0.5, 2.0)
    base = jnp.clip(jax.random.normal(jax.random.fold_in(keyed, 4), (TOKENS, D), jnp.float32), -4.0, 4.0)
    return (base * row_scale * col_scale).astype(jnp.bfloat16)


def draw_weights(key, part):
    keyed = jax.random.fold_in(key, 2)
    head_index = (jnp.arange(HD, dtype=jnp.int32) // HEAD).astype(jnp.float32)
    fraction = head_index / (HEADS - 1)
    raw = jnp.clip(jax.random.normal(jax.random.fold_in(keyed, 1), (3, D, HD), jnp.float32), -5.0, 5.0)
    ramp = 1.0 + 0.75 * fraction
    query_part = raw[0]
    key_part = raw[1]
    value_part = raw[2]
    scaling = D ** (-0.5)
    stacked = jnp.stack([query_part * ramp[None, :], key_part * ramp[None, :], value_part]) * scaling
    return stacked.astype(jnp.bfloat16)


def block_scale(rng, shape, shards, low, high):
    gain, own = 1.0, jax.random.fold_in(rng, 6)
    for position, blocks in shards:
        heights = jnp.exp(jax.random.uniform(jax.random.fold_in(own, position), (blocks,), jnp.float32, low / len(shards), high / len(shards)))
        gain = gain * jnp.repeat(heights, shape[position] // blocks).reshape([-1 if axis == position else 1 for axis in range(len(shape))])
    return gain


def centred(key, dims, scale, limit, shards=(), kind=jnp.bfloat16):
    entries = scale * jax.random.normal(key, dims, jnp.float32)
    if shards:
        entries = entries * block_scale(key, dims, shards, -0.22, 0.18)
    return jnp.clip(entries, -limit, limit).astype(kind)


def setup_inputs(seed: int = 0, part: int = 0) -> dict:
    arg_keys = jax.random.split(jax.random.key(seed), 9)
    part_keys = jax.random.split(jax.random.fold_in(arg_keys[8], part), 9)
    tokens = draw_tokens(jax.random.fold_in(jax.random.fold_in(arg_keys[8], part), 71), part)
    weights = draw_weights(jax.random.fold_in(arg_keys[8], 71), part)
    modulation = centred(part_keys[2], (2, CLIPS, D), 0.5, 3.0, (), jnp.float32)
    qk_gain = jnp.clip(1.0 + 0.15 * jax.random.normal(arg_keys[3], (2, HD), jnp.float32), 0.25, 1.75)
    segment_ids = draw_segment_ids(jax.random.fold_in(jax.random.fold_in(arg_keys[8], part), 71), part)
    positions = draw_positions(jax.random.fold_in(jax.random.fold_in(arg_keys[8], part), 71), part)
    page_table = draw_page_table(jax.random.fold_in(jax.random.fold_in(arg_keys[8], part), 71), part)
    kv_cache = centred(part_keys[7], (2, HEADS, POOL, PAGE, HEAD), 1.0, 6.0, ((1, 8),))
    return {"tokens": tokens, "weights": weights, "modulation": modulation, "qk_gain": qk_gain, "segment_ids": segment_ids, "positions": positions, "page_table": page_table, "kv_cache": kv_cache}


epsilon = 1e-06
masked_score = -1e+30

def rotary_tables(positions, head_size):
    height_dims = 2 * (head_size // 6)
    frame_dims = head_size - 2 * height_dims
    frame_freq = 1.0 / 10000.0 ** (np.arange(0, frame_dims, 2) / frame_dims)
    height_freq = 1.0 / 10000.0 ** (np.arange(0, height_dims, 2) / height_dims)
    zero_frame = np.zeros(frame_dims // 2)
    zero_height = np.zeros(height_dims // 2)
    table_frame = np.concatenate([frame_freq, zero_height, zero_height])
    table_height = np.concatenate([zero_frame, height_freq, zero_height])
    table_width = np.concatenate([zero_frame, zero_height, height_freq])
    coords = positions.astype(jnp.float32)
    angles = coords[0][:, None] * jnp.asarray(table_frame, jnp.float32)[None, :]
    angles = angles + coords[1][:, None] * jnp.asarray(table_height, jnp.float32)[None, :]
    angles = angles + coords[2][:, None] * jnp.asarray(table_width, jnp.float32)[None, :]
    return (jnp.cos(angles), jnp.sin(angles))

def rotary_apply(channels, cosine, sine_table):
    first = channels[..., 0::2]
    second = channels[..., 1::2]
    cos_rows = cosine[:, None, :]
    sin_rows = sine_table[:, None, :]
    turned = jnp.stack([first * cos_rows - second * sin_rows, first * sin_rows + second * cos_rows], axis=-1)
    return turned.reshape(channels.shape)

def layer_norm_mod(rows, seg_rows, modulation):
    floats = rows.astype(jnp.float32)
    center = floats - lax.optimization_barrier(jnp.mean(floats, axis=1, keepdims=True))
    spread = lax.optimization_barrier(jnp.mean(center * center, axis=1, keepdims=True))
    normed = center * lax.rsqrt(spread + epsilon)
    onehot = (seg_rows[:, None] == jnp.arange(modulation.shape[1], dtype=jnp.int32)[None, :]).astype(jnp.float32)
    shifts = jnp.dot(onehot, modulation[0], precision=lax.Precision.HIGHEST)
    scales = jnp.dot(onehot, modulation[1], precision=lax.Precision.HIGHEST)
    return (normed * (1.0 + scales) + shifts).astype(jnp.bfloat16)

def reference(tokens, weights, modulation, qk_gain, segment_ids, positions, page_table, kv_cache):
    x_mod = layer_norm_mod(tokens, segment_ids, modulation)
    queries = jnp.dot(x_mod, weights[0], preferred_element_type=jnp.float32)
    key_rows = jnp.dot(x_mod, weights[1], preferred_element_type=jnp.float32)
    values = jnp.dot(x_mod, weights[2], preferred_element_type=jnp.float32)
    channels = queries.shape[1]
    q_mean = lax.optimization_barrier(jnp.sum(queries * queries, axis=1)) / channels
    k_mean = lax.optimization_barrier(jnp.sum(key_rows * key_rows, axis=1)) / channels
    cosine, sine_table = rotary_tables(positions, HEAD)
    q_norm = queries * lax.rsqrt(q_mean + epsilon)[:, None] * qk_gain[0][None, :]
    k_norm = key_rows * lax.rsqrt(k_mean + epsilon)[:, None] * qk_gain[1][None, :]
    q_rot = rotary_apply(q_norm.reshape(TOKENS, HEADS, HEAD), cosine, sine_table).astype(jnp.bfloat16)
    k_rot = rotary_apply(k_norm.reshape(TOKENS, HEADS, HEAD), cosine, sine_table).astype(jnp.bfloat16)
    v_low = values.astype(jnp.bfloat16).reshape(TOKENS, HEADS, HEAD)
    is_valid = segment_ids < CLIPS
    allowed = (segment_ids[:, None] == segment_ids[None, :]) & is_valid[:, None]
    scaling = float(HEAD) ** (-0.5)

    def per_head(operands):
        q_head, k_head, v_head = operands
        scores = jnp.dot(q_head, k_head.T, preferred_element_type=jnp.float32) * scaling
        scores = jnp.where(allowed, scores, masked_score)
        row_top = lax.optimization_barrier(jnp.max(scores, axis=1, keepdims=True))
        exponent = jnp.exp(scores - row_top)
        row_total = lax.optimization_barrier(jnp.sum(exponent, axis=1, keepdims=True))
        probabilities = exponent.astype(jnp.bfloat16)
        result = jnp.dot(probabilities, v_head, preferred_element_type=jnp.float32) / row_total
        return jnp.where(is_valid[:, None], result, 0.0).astype(jnp.bfloat16)
    heads_out = lax.map(per_head, (q_rot.transpose(1, 0, 2), k_rot.transpose(1, 0, 2), v_low.transpose(1, 0, 2)))
    attended = heads_out.transpose(1, 0, 2).reshape(TOKENS, HEADS * HEAD)
    stacked = jnp.stack([k_rot, v_low]).reshape(2, NPAGES, PAGE, HEADS, HEAD)
    paged = stacked.transpose(0, 3, 1, 2, 4)
    new_cache = kv_cache.at[:, :, page_table].set(paged)
    return (attended, new_cache)
```

```python
import functools

import jax
import jax.numpy as jnp
import numpy as np
from jax import lax
from jax.experimental import pallas as pl
from jax.experimental.pallas import tpu as pltpu
from jax.sharding import PartitionSpec as P

HEAD = 128
HEADS = 32
PAGE = 16
EPS = 1e-6
MASKED = -1e30
F32 = jnp.float32
BF16 = jnp.bfloat16
VMEM = pltpu.VMEM
SMEM = pltpu.SMEM
ANY = pl.ANY


def ring_order(n):
    nx = 1
    while 2 * nx * nx < n:
        nx *= 2
    nz = n // nx
    if nx == 1:
        return list(range(n))
    order = []
    for z in range(nz):
        xs = range(1, nx)
        order += [z * nx + x for x in (xs if z % 2 == 0 else reversed(xs))]
    order += [z * nx for z in reversed(range(nz))]
    if nz % 2:
        return list(range(n))
    return order


def half_rows(rows):
    first = (rows // 2 + 15) // 16 * 16
    return (first, rows - first)


def signed_tables(positions, row_count):
    height_dims = 2 * (HEAD // 6)
    frame_dims = HEAD - 2 * height_dims
    frame_freq = 1.0 / 10000.0 ** (np.arange(0, frame_dims, 2) / frame_dims)
    height_freq = 1.0 / 10000.0 ** (np.arange(0, height_dims, 2) / height_dims)
    zero_frame = np.zeros(frame_dims // 2)
    zero_height = np.zeros(height_dims // 2)
    tables = [
        np.concatenate([frame_freq, zero_height, zero_height]),
        np.concatenate([zero_frame, height_freq, zero_height]),
        np.concatenate([zero_frame, zero_height, height_freq]),
    ]
    tables = [np.repeat(t, 2).astype(np.float32) for t in tables]
    sign = np.where(np.arange(HEAD) % 2 == 0, -1.0, 1.0).astype(np.float32)
    coords = positions.astype(F32)
    angles = coords[0][:, None] * jnp.asarray(tables[0])[None, :]
    angles = angles + coords[1][:, None] * jnp.asarray(tables[1])[None, :]
    angles = angles + coords[2][:, None] * jnp.asarray(tables[2])[None, :]
    cosine = jnp.cos(angles)
    sine = jnp.sin(angles) * jnp.asarray(sign)[None, :]
    return jnp.stack([cosine, sine]).reshape(2, -1, row_count, HEAD)


def ln_kernel(seg_ref, tok_ref, mod_ref, out_ref, *, clips):
    rows = tok_ref.shape[0]
    x = tok_ref[...].astype(F32)
    inv = 1.0 / x.shape[1]
    center = x - jnp.sum(x, axis=1, keepdims=True) * inv
    spread = jnp.sum(center * center, axis=1, keepdims=True) * inv
    normed = center * lax.rsqrt(spread + EPS)
    seg = seg_ref[...]
    classes = lax.broadcasted_iota(jnp.int32, (16, rows), 0)
    hot = jnp.where(classes == seg, 1.0, 0.0).astype(BF16)
    hot = jnp.concatenate([hot] * 3, axis=0)

    def pick(which):
        table = mod_ref[:, which, :]
        table = jnp.concatenate([table, jnp.zeros((16 - clips, table.shape[1]), F32)], axis=0)
        high = table.astype(BF16)
        rest = table - high.astype(F32)
        mid = rest.astype(BF16)
        low = (rest - mid.astype(F32)).astype(BF16)
        stacked = jnp.concatenate([high, mid, low], axis=0)
        return lax.dot_general(
            hot, stacked, (((0,), (0,)), ((), ())), preferred_element_type=F32
        )

    out_ref[...] = (normed * (1.0 + pick(1)) + pick(0)).astype(BF16)


def modulated(tokens, seg_rows, mod, clips, start, rows):
    width = tokens.shape[1]
    return pl.pallas_call(
        functools.partial(ln_kernel, clips=clips),
        out_shape=jax.ShapeDtypeStruct((rows, width), BF16),
        grid=(1,),
        in_specs=[
            pl.BlockSpec((1, rows), lambda i: (0, 0)),
            pl.BlockSpec((rows, width), lambda i: (0, 0)),
            pl.BlockSpec(mod.shape, lambda i: (0, 0, 0)),
        ],
        out_specs=pl.BlockSpec((rows, width), lambda i: (0, 0)),
        cost_estimate=pl.CostEstimate(
            flops=20 * rows * width, transcendentals=0, bytes_accessed=4 * rows * width
        ),
        name="ln",
    )(seg_rows[:, start : start + rows], tokens[start : start + rows], mod)


def rotate(y, cosine, sine):
    lane = lax.broadcasted_iota(jnp.int32, y.shape, 1)
    left = pltpu.roll(y, HEAD - 1, 1)
    right = pltpu.roll(y, 1, 1)
    swapped = jnp.where(lane % 2 == 0, left, right)
    return y * cosine + swapped * sine


def qkv_kernel(idx_ref, *refs, sizes, block):
    count = len(sizes)
    x_refs = refs[:count]
    w_ref, gain_ref, trig_ref, sq_in_ref, y_ref, sq_ref, x_sc = refs[count:]
    which = pl.program_id(0)
    part = pl.program_id(1)
    starts = [sum(sizes[:i]) for i in range(count)]
    total = sum(sizes)

    @pl.when((which == 0) & (part == 0))
    def _():
        for x_ref, start, size in zip(x_refs, starts, sizes):
            x_sc[start : start + size, :] = x_ref[...]
        sq_ref[...] = sq_in_ref[...]
        for u in range(count):
            sq_ref[idx_ref[2 * u + 1]] = jnp.zeros((2, 128), F32)

    y = jnp.dot(x_sc[...], w_ref[0], preferred_element_type=F32)

    @pl.when(which == 2)
    def _():
        y_ref[0] = y

    @pl.when(which < 2)
    def _():
        gain = gain_ref[0]
        for u, (start, size) in enumerate(zip(starts, sizes)):
            row = pl.multiple_of(idx_ref[2 * u], 16)
            cosine = trig_ref[0, pl.ds(row, size), :]
            sine = trig_ref[1, pl.ds(row, size), :]
            squares = jnp.zeros((size, HEAD), F32)
            for h in range(block // HEAD):
                cols = slice(h * HEAD, (h + 1) * HEAD)
                piece = y[start : start + size, cols]
                squares = squares + piece * piece
                y_ref[0, start : start + size, cols] = rotate(
                    piece * gain[:, cols], cosine, sine
                )
            padded = jnp.concatenate(
                [squares, jnp.zeros((128 - size, HEAD), F32)], axis=0
            )
            sums = jnp.sum(padded.T, axis=0, keepdims=True)
            unit = idx_ref[2 * u + 1]
            sq_ref[unit, pl.ds(which, 1), :] = sq_ref[unit, pl.ds(which, 1), :] + sums


def qkv_chunk(idx, xs, weights, gain, trig, sq):
    sizes = tuple(x.shape[0] for x in xs)
    total = sum(sizes)
    _, width, cols = weights.shape
    block = min(256, cols)
    grid = (3, cols // block)
    return pl.pallas_call(
        functools.partial(qkv_kernel, sizes=sizes, block=block),
        out_shape=(
            jax.ShapeDtypeStruct((3, total, cols), F32),
            jax.ShapeDtypeStruct(sq.shape, F32),
        ),
        grid_spec=pltpu.PrefetchScalarGridSpec(
            num_scalar_prefetch=1,
            grid=grid,
            in_specs=[pl.BlockSpec((s, width), lambda i, j, idx: (0, 0)) for s in sizes]
            + [
                pl.BlockSpec((1, width, block), lambda i, j, idx: (i, 0, j)),
                pl.BlockSpec((1, 1, block), lambda i, j, idx: (jnp.minimum(i, 1), 0, j)),
                pl.BlockSpec(trig.shape, lambda i, j, idx: (0, 0, 0)),
                pl.BlockSpec(sq.shape, lambda i, j, idx: (0, 0, 0)),
            ],
            out_specs=(
                pl.BlockSpec((1, total, block), lambda i, j, idx: (i, 0, j)),
                pl.BlockSpec(sq.shape, lambda i, j, idx: (0, 0, 0)),
            ),
            scratch_shapes=[VMEM((total, width), BF16)],
        ),
        cost_estimate=pl.CostEstimate(
            flops=2 * total * width * cols * 3,
            transcendentals=0,
            bytes_accessed=weights.size * 2 + total * width * 2 + total * cols * 12,
        ),
        compiler_params=pltpu.CompilerParams(vmem_limit_bytes=24 << 20),
        name="qkv",
    )(idx, *xs, weights, gain, trig, sq)


def attention(order_idx, totals, segcol, segrow, ys, layout, long, n, rows, channels, clips):
    total, cols = n * rows, ys[0].shape[2]
    heads = cols // HEAD
    scale = float(HEAD) ** -0.5
    qblock = 256 if long % 256 == 0 else long

    def kernel(idx_ref, sq_ref, segcol_ref, segrow_ref, *refs):
        y_refs = refs[: len(ys)]
        out_refs = refs[len(ys) : len(ys) + n]
        kv_ref, q_sc, att_sc = refs[len(ys) + n :]
        units = sq_ref.shape[0]
        inv = lax.rsqrt(sq_ref[...] * (1.0 / channels) + EPS).reshape(2 * units, 128)
        pad = (-2 * units) % 128
        if pad:
            inv = jnp.concatenate([inv, jnp.zeros((pad, 128), F32)], axis=0)
        cols_t = inv.T
        lane = lax.broadcasted_iota(jnp.int32, cols_t.shape, 1)
        at = 0
        for y_ref, sizes in zip(y_refs, layout):
            start = 0
            for size in sizes:
                row = pl.multiple_of(idx_ref[2 * at], 16)
                unit = idx_ref[2 * at + 1]
                r_q = jnp.sum(jnp.where(lane == 2 * unit, cols_t, 0.0), axis=1, keepdims=True)
                r_k = jnp.sum(jnp.where(lane == 2 * unit + 1, cols_t, 0.0), axis=1, keepdims=True)
                here = slice(start, start + size)
                q_sc[pl.ds(row, size), :] = (y_ref[0, here, :] * r_q[:size]).astype(BF16)
                kv_ref[0, pl.ds(row, size), :] = (y_ref[1, here, :] * r_k[:size]).astype(BF16)
                kv_ref[1, pl.ds(row, size), :] = y_ref[2, here, :].astype(BF16)
                start += size
                at += 1

        def attend(q_rows, k_rows, lanes, masked):
            q = q_sc[q_rows, lanes]
            k = kv_ref[0, k_rows, lanes]
            v = kv_ref[1, k_rows, lanes]
            s = lax.dot_general(q, k, (((1,), (1,)), ((), ())), preferred_element_type=F32)
            s = s * scale
            if masked:
                seg_q = segcol_ref[q_rows, :]
                allowed = (seg_q == segrow_ref[:, k_rows]) & (seg_q < clips)
                s = jnp.where(allowed, s, MASKED)
            top = jnp.max(s, axis=1, keepdims=True)
            e = jnp.exp(s - top)
            denom = jnp.sum(e, axis=1, keepdims=True)
            o = jnp.dot(e.astype(BF16), v, preferred_element_type=F32) / denom
            if masked:
                o = jnp.where(seg_q < clips, o, 0.0)
            att_sc[q_rows, lanes] = o.astype(BF16)

        for h in range(heads):
            lanes = slice(h * HEAD, (h + 1) * HEAD)
            for start in range(0, long, qblock):
                attend(slice(start, start + qblock), slice(0, long), lanes, False)
            attend(slice(long, total), slice(long, total), lanes, True)
        me = idx_ref[2 * at]
        for o in range(n):
            row = pl.multiple_of((me ^ o) * rows, 16)
            out_refs[o][...] = att_sc[pl.ds(row, rows), :]

    whole = pl.BlockSpec(memory_space=VMEM)
    return pl.pallas_call(
        kernel,
        out_shape=tuple([jax.ShapeDtypeStruct((rows, cols), BF16)] * n)
        + (jax.ShapeDtypeStruct((2, total, cols), BF16),),
        in_specs=[pl.BlockSpec(memory_space=SMEM)] + [whole] * (3 + len(ys)),
        out_specs=tuple([whole] * (n + 1)),
        scratch_shapes=[VMEM((total, cols), BF16), VMEM((total, cols), BF16)],
        cost_estimate=pl.CostEstimate(
            flops=4 * total * long * cols,
            transcendentals=heads * long * total,
            bytes_accessed=total * cols * 20,
        ),
        compiler_params=pltpu.CompilerParams(vmem_limit_bytes=40 << 20),
        name="attend",
    )(order_idx, totals, segcol, segrow, *ys)


def cache_write(page_table, kv_cache, kv):
    _, heads, pool, page, head = kv_cache.shape
    total = kv.shape[1]

    def kernel(pt_ref, cache_ref, kv_ref, out_ref):
        out_ref[...] = cache_ref[...]

        def step(i, carry):
            row = pl.multiple_of(i * page, page)
            out_ref[0, 0, pt_ref[i]] = kv_ref[0, pl.ds(row, page), :]
            return carry

        lax.fori_loop(0, total // page, step, 0)

    return pl.pallas_call(
        kernel,
        out_shape=jax.ShapeDtypeStruct(kv_cache.shape, BF16),
        grid_spec=pltpu.PrefetchScalarGridSpec(
            num_scalar_prefetch=1,
            grid=(2, heads),
            in_specs=[
                pl.BlockSpec((1, 1, pool, page, head), lambda i, h, pt: (i, h, 0, 0, 0)),
                pl.BlockSpec((1, total, head), lambda i, h, pt: (i, 0, h)),
            ],
            out_specs=pl.BlockSpec((1, 1, pool, page, head), lambda i, h, pt: (i, h, 0, 0, 0)),
        ),
        cost_estimate=pl.CostEstimate(
            flops=0, transcendentals=0, bytes_accessed=kv_cache.size * 4
        ),
        name="cache",
    )(page_table, kv_cache, kv)


def assemble(me, parts):
    n = len(parts)
    rows, cols = parts[0].shape

    def kernel(me_ref, *refs):
        out_ref = refs[n]
        for o in range(n):
            col = pl.multiple_of((me_ref[0] ^ o) * cols, 128)
            out_ref[:, pl.ds(col, cols)] = refs[o][...]

    whole = pl.BlockSpec(memory_space=VMEM)
    return pl.pallas_call(
        kernel,
        out_shape=jax.ShapeDtypeStruct((rows, n * cols), BF16),
        in_specs=[pl.BlockSpec(memory_space=SMEM)] + [whole] * n,
        out_specs=whole,
        name="assemble",
    )(me, *parts)


def body(tokens, weights, modulation, qk_gain, segment_ids, positions, page_table, kv_cache, *, n):
    rows = tokens.shape[0]
    total = n * rows
    long = total * 4 // 5
    clips = modulation.shape[1]
    me = lax.axis_index("tp")
    sizes = half_rows(rows)
    order = ring_order(n)
    place = np.argsort(np.array(order))
    fwd = [(order[i], order[(i + 1) % n]) for i in range(n)]
    bwd = [(b, a) for a, b in fwd]
    order_arr = np.array(order, np.int32)
    my_place = jnp.asarray(place.astype(np.int32))[me]

    def source(step):
        return jnp.asarray(order_arr)[(my_place - step) % n]

    def unit_idx(src, half):
        return [src * rows + (sizes[0] if half else 0), 2 * src + half]

    mod = modulation.transpose(1, 0, 2)
    own_seg = lax.dynamic_slice_in_dim(segment_ids, me * rows, rows).reshape(1, rows)
    halves = [
        modulated(tokens, own_seg, mod, clips, 0, sizes[0]),
        modulated(tokens, own_seg, mod, clips, sizes[0], sizes[1]),
    ]
    trig = signed_tables(positions, total).reshape(2, total, HEAD)
    gain = qk_gain.reshape(2, 1, -1)
    sq = jnp.zeros((2 * n, 2, 128), F32)

    chunks = [(list(halves), [(0, 0), (0, 1)])]
    cw, ccw = list(halves), list(halves)
    steps = n // 2
    for s in range(1, steps):
        for j in range(2):
            cw[j] = lax.ppermute(cw[j], "tp", fwd)
            ccw[j] = lax.ppermute(ccw[j], "tp", bwd)
            chunks.append(([cw[j], ccw[j]], [(s, j), (-s, j)]))
    last_a = lax.ppermute(cw[0], "tp", fwd)
    last_b = lax.ppermute(ccw[1], "tp", bwd)
    chunks.append(([last_a, last_b], [(steps, 0), (-steps, 1)]))

    ys, layout, all_idx = [], [], []
    for xs, units in chunks:
        flat = []
        for s, j in units:
            flat += unit_idx(source(s), j)
        idx = jnp.stack(flat).astype(jnp.int32)
        y, sq = qkv_chunk(idx, xs, weights, gain, trig, sq)
        ys.append(y)
        layout.append(tuple(x.shape[0] for x in xs))
        all_idx += flat
    hop = 1
    while hop < n:
        sq = sq + lax.ppermute(sq, "tp", [(i, i ^ hop) for i in range(n)])
        hop *= 2
    order_idx = jnp.stack(all_idx + [me]).astype(jnp.int32)
    res = attention(
        order_idx,
        sq,
        segment_ids.reshape(total, 1),
        segment_ids.reshape(1, total),
        ys,
        layout,
        long,
        n,
        rows,
        HEADS * HEAD,
        clips,
    )
    outs, kv = res[:n], res[n]
    parts = [outs[0]] + [None] * (n - 1)
    for o in reversed(range(1, n)):
        parts[o] = lax.ppermute(outs[o], "tp", [(i, i ^ o) for i in range(n)])
    new_cache = cache_write(page_table, kv_cache, kv)
    attended = assemble(me.reshape(1).astype(jnp.int32), parts)
    return (attended, new_cache)


def solution(mesh):
    return jax.shard_map(
        functools.partial(body, n=mesh.shape["tp"]),
        mesh=mesh,
        in_specs=(
            P(("rep", "tp"), None),
            P(None, None, "tp"),
            P(None, "rep", None),
            P(None, "tp"),
            P("rep"),
            P(None, "rep"),
            P("rep"),
            P(None, "tp", "rep", None, None),
        ),
        out_specs=(P(("rep", "tp"), None), P(None, "tp", "rep", None, None)),
        check_vma=False,
    )
```

```python
import functools

import jax
import jax.numpy as jnp
import numpy as np
from jax import lax
from jax.experimental import pallas as pl
from jax.experimental.pallas import tpu as pltpu
from jax.sharding import PartitionSpec as P


HEAD = 128
HEADS = 32
PAGE = 16
EPS = 1e-6
MASKED = -1e30
F32 = jnp.float32
BF16 = jnp.bfloat16
VMEM = pltpu.VMEM
SMEM = pltpu.SMEM
ANY = pl.ANY


def ring_order(n):
    nx = 1
    while 2 * nx * nx < n:
        nx *= 2
    nz = n // nx
    if nx == 1:
        return list(range(n))
    order = []
    for z in range(nz):
        xs = range(1, nx)
        order += [z * nx + x for x in (xs if z % 2 == 0 else reversed(xs))]
    order += [z * nx for z in reversed(range(nz))]
    if nz % 2:
        return list(range(n))
    return order


def half_rows(rows):
    first = (rows // 2 + 15) // 16 * 16
    return (first, rows - first)


def signed_tables(positions, row_count):
    height_dims = 2 * (HEAD // 6)
    frame_dims = HEAD - 2 * height_dims
    frame_freq = 1.0 / 10000.0 ** (np.arange(0, frame_dims, 2) / frame_dims)
    height_freq = 1.0 / 10000.0 ** (np.arange(0, height_dims, 2) / height_dims)
    zero_frame = np.zeros(frame_dims // 2)
    zero_height = np.zeros(height_dims // 2)
    tables = [
        np.concatenate([frame_freq, zero_height, zero_height]),
        np.concatenate([zero_frame, height_freq, zero_height]),
        np.concatenate([zero_frame, zero_height, height_freq]),
    ]
    tables = [np.repeat(t, 2).astype(np.float32) for t in tables]
    sign = np.where(np.arange(HEAD) % 2 == 0, -1.0, 1.0).astype(np.float32)
    coords = positions.astype(F32)
    angles = coords[0][:, None] * jnp.asarray(tables[0])[None, :]
    angles = angles + coords[1][:, None] * jnp.asarray(tables[1])[None, :]
    angles = angles + coords[2][:, None] * jnp.asarray(tables[2])[None, :]
    cosine = jnp.cos(angles)
    sine = jnp.sin(angles) * jnp.asarray(sign)[None, :]
    return jnp.stack([cosine, sine]).reshape(2, -1, row_count, HEAD)


def ln_kernel(seg_ref, tok_ref, mod_ref, out_ref, x_sc, sem, *, clips, start, rows, all_rows, n):
    copy = pltpu.make_async_copy(tok_ref.at[pl.ds(start, rows)], x_sc, sem)
    copy.start()
    me = lax.axis_index("tp")
    seg = jnp.zeros((1, rows), jnp.int32)
    for b in range(n):
        at = b * all_rows + start
        seg = jnp.where(me == b, seg_ref[:, at : at + rows], seg)
    classes = lax.broadcasted_iota(jnp.int32, (16, rows), 0)
    hot = jnp.where(classes == seg, 1.0, 0.0).astype(BF16)
    hot = jnp.concatenate([hot] * 3, axis=0)

    def pick(which):
        table = mod_ref[:, which, :]
        table = jnp.concatenate([table, jnp.zeros((16 - clips, table.shape[1]), F32)], axis=0)
        high = table.astype(BF16)
        rest = table - high.astype(F32)
        mid = rest.astype(BF16)
        low = (rest - mid.astype(F32)).astype(BF16)
        stacked = jnp.concatenate([high, mid, low], axis=0)
        return lax.dot_general(
            hot, stacked, (((0,), (0,)), ((), ())), preferred_element_type=F32
        )

    scale = 1.0 + pick(1)
    shift = pick(0)
    copy.wait()
    x = x_sc[...].astype(F32)
    inv = 1.0 / x.shape[1]
    center = x - jnp.sum(x, axis=1, keepdims=True) * inv
    spread = jnp.sum(center * center, axis=1, keepdims=True) * inv
    normed = center * lax.rsqrt(spread + EPS)
    out_ref[...] = (normed * scale + shift).astype(BF16)


def modulated(tokens, seg_row, mod, clips, start, rows, n):
    all_rows, width = tokens.shape
    whole = pl.BlockSpec(memory_space=VMEM)
    return pl.pallas_call(
        functools.partial(
            ln_kernel, clips=clips, start=start, rows=rows, all_rows=all_rows, n=n
        ),
        out_shape=jax.ShapeDtypeStruct((rows, width), BF16),
        in_specs=[whole, pl.BlockSpec(memory_space=ANY), whole],
        out_specs=whole,
        scratch_shapes=[VMEM((rows, width), BF16), pltpu.SemaphoreType.DMA],
        cost_estimate=pl.CostEstimate(
            flops=20 * rows * width, transcendentals=0, bytes_accessed=4 * rows * width
        ),
        compiler_params=pltpu.CompilerParams(vmem_limit_bytes=16 << 20),
        name="ln",
    )(seg_row, tokens, mod)


def rotate(y, cosine, sine):
    lane = lax.broadcasted_iota(jnp.int32, y.shape, 1)
    left = pltpu.roll(y, HEAD - 1, 1)
    right = pltpu.roll(y, 1, 1)
    swapped = jnp.where(lane % 2 == 0, left, right)
    return y * cosine + swapped * sine


def qkv_kernel(idx_ref, *refs, sizes, block, base, first):
    count = len(sizes)
    x_refs = refs[:count]
    w_ref, gain_ref, trig_ref, sq_in_ref, y_ref, sq_ref, x_sc = refs[count:]
    step = pl.program_id(0)
    which = step + first
    part = pl.program_id(1)
    starts = [sum(sizes[:i]) for i in range(count)]

    @pl.when((step == 0) & (part == 0))
    def _():
        for x_ref, start, size in zip(x_refs, starts, sizes):
            x_sc[start : start + size, :] = x_ref[...]
        sq_ref[...] = sq_in_ref[...]
        if first == 0:
            for u in range(count):
                sq_ref[idx_ref[base + 2 * u + 1]] = jnp.zeros((2, 128), F32)

    cols_at = pl.ds(pl.multiple_of(part * block, 128), block)
    y = jnp.dot(x_sc[...], w_ref[which, :, cols_at], preferred_element_type=F32)

    @pl.when(which == 2)
    def _():
        y_ref[0] = y

    @pl.when(which < 2)
    def _():
        gain = gain_ref[0]
        for u, (start, size) in enumerate(zip(starts, sizes)):
            row = pl.multiple_of(idx_ref[base + 2 * u], 16)
            cosine = trig_ref[0, pl.ds(row, size), :]
            sine = trig_ref[1, pl.ds(row, size), :]
            squares = jnp.zeros((size, HEAD), F32)
            for h in range(block // HEAD):
                cols = slice(h * HEAD, (h + 1) * HEAD)
                piece = y[start : start + size, cols]
                squares = squares + piece * piece
                y_ref[0, start : start + size, cols] = rotate(
                    piece * gain[:, cols], cosine, sine
                )
            padded = jnp.concatenate(
                [squares, jnp.zeros((128 - size, HEAD), F32)], axis=0
            )
            sums = jnp.sum(padded.T, axis=0, keepdims=True)
            unit = idx_ref[base + 2 * u + 1]
            sq_ref[unit, pl.ds(which, 1), :] = sq_ref[unit, pl.ds(which, 1), :] + sums


def qkv_chunk(idx, base, xs, weights, gain, trig, sq, first=0, last=3):
    sizes = tuple(x.shape[0] for x in xs)
    total = sum(sizes)
    _, width, cols = weights.shape
    block = min(256, cols)
    grid = (last - first, cols // block)
    return pl.pallas_call(
        functools.partial(qkv_kernel, sizes=sizes, block=block, base=base, first=first),
        out_shape=(
            jax.ShapeDtypeStruct((last - first, total, cols), F32),
            jax.ShapeDtypeStruct(sq.shape, F32),
        ),
        grid_spec=pltpu.PrefetchScalarGridSpec(
            num_scalar_prefetch=1,
            grid=grid,
            in_specs=[pl.BlockSpec(memory_space=VMEM)] * len(sizes)
            + [
                pl.BlockSpec(memory_space=VMEM),
                pl.BlockSpec((1, 1, block), lambda i, j, idx: (jnp.minimum(i + first, 1), 0, j)),
                pl.BlockSpec(memory_space=VMEM),
                pl.BlockSpec(sq.shape, lambda i, j, idx: (0, 0, 0)),
            ],
            out_specs=(
                pl.BlockSpec((1, total, block), lambda i, j, idx: (i, 0, j)),
                pl.BlockSpec(sq.shape, lambda i, j, idx: (0, 0, 0)),
            ),
            scratch_shapes=[VMEM((total, width), BF16)],
        ),
        cost_estimate=pl.CostEstimate(
            flops=2 * total * width * cols * (last - first),
            transcendentals=0,
            bytes_accessed=weights.size * 2 + total * width * 2 + total * cols * 12,
        ),
        compiler_params=pltpu.CompilerParams(vmem_limit_bytes=12 << 20),
        name="qkv",
    )(idx, *xs, weights, gain, trig, sq)


def attention(order_idx, totals, segcol, segrow, ys, layout, long, n, rows, channels, clips):
    total, cols = n * rows, ys[0].shape[2]
    heads = cols // HEAD
    scale = float(HEAD) ** -0.5
    qblock = 256 if long % 256 == 0 else long

    def kernel(idx_ref, sq_ref, segcol_ref, segrow_ref, *refs):
        y_refs = refs[: len(ys) - 1]
        v_last = refs[len(ys) - 1]
        out_refs = refs[len(ys) : len(ys) + n]
        kv_ref, q_sc, att_sc = refs[len(ys) + n :]

        def v_at(y_ref, here):
            return y_ref[2, here, :] if y_ref.shape[0] == 3 else v_last[0, here, :]

        units = sq_ref.shape[0]
        inv = lax.rsqrt(sq_ref[...] * (1.0 / channels) + EPS).reshape(2 * units, 128)
        pad = (-2 * units) % 128
        if pad:
            inv = jnp.concatenate([inv, jnp.zeros((pad, 128), F32)], axis=0)
        cols_t = inv.T
        lane = lax.broadcasted_iota(jnp.int32, cols_t.shape, 1)
        at = 0
        for y_ref, sizes in zip(y_refs, layout):
            start = 0
            for size in sizes:
                row = pl.multiple_of(idx_ref[2 * at], 16)
                unit = idx_ref[2 * at + 1]
                r_q = jnp.sum(jnp.where(lane == 2 * unit, cols_t, 0.0), axis=1, keepdims=True)
                r_k = jnp.sum(jnp.where(lane == 2 * unit + 1, cols_t, 0.0), axis=1, keepdims=True)
                here = slice(start, start + size)
                q_sc[pl.ds(row, size), :] = (y_ref[0, here, :] * r_q[:size]).astype(BF16)
                k_new = (y_ref[1, here, :] * r_k[:size]).astype(BF16)
                v_new = v_at(y_ref, here).astype(BF16)
                for g in range(size // PAGE):
                    block = row // PAGE + g
                    for h in range(heads):
                        piece = (slice(g * PAGE, (g + 1) * PAGE), slice(h * HEAD, (h + 1) * HEAD))
                        kv_ref[0, block, h] = k_new[piece]
                        kv_ref[1, block, h] = v_new[piece]
                start += size
                at += 1

        def attend(q_rows, k_rows, h, masked):
            lanes = slice(h * HEAD, (h + 1) * HEAD)
            pages = slice(k_rows.start // PAGE, k_rows.stop // PAGE)
            q = q_sc[q_rows, lanes]
            k = kv_ref[0, pages, h].reshape(-1, HEAD)
            v = kv_ref[1, pages, h].reshape(-1, HEAD)
            s = lax.dot_general(q, k, (((1,), (1,)), ((), ())), preferred_element_type=F32)
            s = s * scale
            if masked:
                seg_q = segcol_ref[q_rows, :]
                allowed = (seg_q == segrow_ref[:, k_rows]) & (seg_q < clips)
                s = jnp.where(allowed, s, MASKED)
            top = jnp.max(s, axis=1, keepdims=True)
            e = jnp.exp(s - top)
            denom = jnp.sum(e, axis=1, keepdims=True)
            o = jnp.dot(e.astype(BF16), v, preferred_element_type=F32) / denom
            if masked:
                o = jnp.where(seg_q < clips, o, 0.0)
            att_sc[q_rows, lanes] = o.astype(BF16)

        for h in range(heads):
            for start in range(0, long, qblock):
                attend(slice(start, start + qblock), slice(0, long), h, False)
            attend(slice(long, total), slice(long, total), h, True)
        me = idx_ref[2 * at]
        for o in range(n):
            row = pl.multiple_of((me ^ o) * rows, 16)
            out_refs[o][...] = att_sc[pl.ds(row, rows), :]

    whole = pl.BlockSpec(memory_space=VMEM)
    return pl.pallas_call(
        kernel,
        out_shape=tuple([jax.ShapeDtypeStruct((rows, cols), BF16)] * n)
        + (jax.ShapeDtypeStruct((2, total // PAGE, heads, PAGE, HEAD), BF16),),
        in_specs=[pl.BlockSpec(memory_space=SMEM)] + [whole] * (3 + len(ys)),
        out_specs=tuple([whole] * (n + 1)),
        scratch_shapes=[VMEM((total, cols), BF16), VMEM((total, cols), BF16)],
        cost_estimate=pl.CostEstimate(
            flops=4 * total * long * cols,
            transcendentals=heads * long * total,
            bytes_accessed=total * cols * 20,
        ),
        compiler_params=pltpu.CompilerParams(vmem_limit_bytes=24 << 20),
        name="attend",
    )(order_idx, totals, segcol, segrow, *ys)


def cache_copy(kv_cache):
    def kernel(in_ref, out_ref, buf, in_sem, out_sem):
        count = buf.shape[0]
        ins = [pltpu.make_async_copy(in_ref.at[i], buf.at[i], in_sem.at[i]) for i in range(count)]
        outs = [pltpu.make_async_copy(buf.at[i], out_ref.at[i], out_sem.at[i]) for i in range(count)]
        for copy in ins:
            copy.start()
        for before, after in zip(ins, outs):
            before.wait()
            after.start()
        for copy in outs:
            copy.wait()

    return pl.pallas_call(
        kernel,
        out_shape=jax.ShapeDtypeStruct(kv_cache.shape, BF16),
        in_specs=[pl.BlockSpec(memory_space=ANY)],
        out_specs=pl.BlockSpec(memory_space=ANY),
        scratch_shapes=[
            VMEM(kv_cache.shape, BF16),
            pltpu.SemaphoreType.DMA((kv_cache.shape[0],)),
            pltpu.SemaphoreType.DMA((kv_cache.shape[0],)),
        ],
        cost_estimate=pl.CostEstimate(
            flops=0, transcendentals=0, bytes_accessed=kv_cache.size * 4
        ),
        compiler_params=pltpu.CompilerParams(vmem_limit_bytes=4 << 20),
    )(kv_cache)


def cache_write(page_table, kv_cache, kv):
    pages = kv.shape[1]

    def kernel(pt_ref, cache_ref, kv_ref, out_ref, sem):
        def copies(p):
            for i in range(2):
                yield pltpu.make_async_copy(
                    kv_ref.at[i, p], out_ref.at[i, :, pt_ref[p]], sem.at[i, p]
                )

        def send(p, carry):
            for copy in copies(p):
                copy.start()
            return carry

        def finish(p, carry):
            for copy in copies(p):
                copy.wait()
            return carry

        lax.fori_loop(0, pages, send, 0)
        lax.fori_loop(0, pages, finish, 0)

    return pl.pallas_call(
        kernel,
        out_shape=jax.ShapeDtypeStruct(kv_cache.shape, BF16),
        in_specs=[
            pl.BlockSpec(memory_space=SMEM),
            pl.BlockSpec(memory_space=ANY),
            pl.BlockSpec(memory_space=VMEM),
        ],
        out_specs=pl.BlockSpec(memory_space=ANY),
        scratch_shapes=[pltpu.SemaphoreType.DMA((2, pages))],
        input_output_aliases={1: 0},
        cost_estimate=pl.CostEstimate(
            flops=0, transcendentals=0, bytes_accessed=kv.size * 4
        ),
        compiler_params=pltpu.CompilerParams(vmem_limit_bytes=4 << 20),
        name="cache",
    )(page_table, kv_cache, kv)


def assemble(idx, parts):
    n = len(parts)
    rows, cols = parts[0].shape

    last = idx.shape[0] - 1

    def kernel(idx_ref, *refs):
        out_ref = refs[n]
        for o in range(n):
            col = pl.multiple_of((idx_ref[last] ^ o) * cols, 128)
            out_ref[:, pl.ds(col, cols)] = refs[o][...]

    whole = pl.BlockSpec(memory_space=VMEM)
    return pl.pallas_call(
        kernel,
        out_shape=jax.ShapeDtypeStruct((rows, n * cols), BF16),
        in_specs=[pl.BlockSpec(memory_space=SMEM)] + [whole] * n,
        out_specs=whole,
        cost_estimate=pl.CostEstimate(
            flops=0, transcendentals=0, bytes_accessed=4 * n * rows * cols
        ),
        compiler_params=pltpu.CompilerParams(vmem_limit_bytes=4 << 20),
        name="assemble",
    )(idx, *parts)


def body(tokens, weights, modulation, qk_gain, segment_ids, positions, page_table, kv_cache, *, n):
    rows = tokens.shape[0]
    total = n * rows
    long = total * 4 // 5
    clips = modulation.shape[1]
    me = lax.axis_index("tp")
    sizes = half_rows(rows)
    order = ring_order(n)
    place = np.argsort(np.array(order))
    fwd = [(order[i], order[(i + 1) % n]) for i in range(n)]
    bwd = [(b, a) for a, b in fwd]
    steps = n // 2
    units = [[(0, 0), (0, 1)]]
    for s in range(1, steps):
        units += [[(s, j), (-s, j)] for j in range(2)]
    units.append([(steps, 0), (-steps, 1)])
    flat = [u for chunk in units for u in chunk]
    table = np.zeros((n, 2 * len(flat) + 1), np.int32)
    for d in range(n):
        for i, (s, j) in enumerate(flat):
            src = order[(place[d] - s) % n]
            table[d, 2 * i] = src * rows + (sizes[0] if j else 0)
            table[d, 2 * i + 1] = 2 * src + j
        table[d, -1] = d
    idx = lax.dynamic_index_in_dim(jnp.asarray(table), me, 0, keepdims=False)

    mod = modulation.transpose(1, 0, 2)
    seg_row = segment_ids.reshape(1, total)
    halves = [
        modulated(tokens, seg_row, mod, clips, 0, sizes[0], n),
        modulated(tokens, seg_row, mod, clips, sizes[0], sizes[1], n),
    ]
    trig = signed_tables(positions, total).reshape(2, total, HEAD)
    gain = qk_gain.reshape(2, 1, -1)
    sq = jnp.zeros((2 * n, 2, 128), F32)

    ys, layout = [], []
    state = {"sq": sq, "base": 0}

    def project(xs):
        y, state["sq"] = qkv_chunk(
            idx, state["base"], xs, weights, gain, trig, state["sq"]
        )
        state["base"] += 2 * len(xs)
        ys.append(y)
        layout.append(tuple(x.shape[0] for x in xs))

    def gate(a, b):
        a, b, state["sq"] = lax.optimization_barrier((a, b, state["sq"]))
        return a, b

    def hop(x, pairs):
        return lax.ppermute(x, "tp", pairs)

    def hop_pair(a, b):
        return hop(a, fwd), hop(b, bwd)

    cw, ccw = [None] * 2, [None] * 2
    for j in range(2):
        cw[j], ccw[j] = hop_pair(halves[j], halves[j])
    project(list(halves))
    for s in range(1, steps):
        for j in range(2):
            a, b = cw[j], ccw[j]
            ga, gb = gate(a, b)
            if s < steps - 1:
                cw[j], ccw[j] = hop_pair(ga, gb)
            elif j == 0:
                last_a = hop(ga, fwd)
            else:
                last_b = hop(gb, bwd)
            if s == 1 and j == 0:
                kv_cache, state["sq"] = lax.optimization_barrier((kv_cache, state["sq"]))
                kv_cache = cache_copy(kv_cache)
            project([a, b])
    last = [last_a, last_b]
    base = state["base"]
    y, sq = qkv_chunk(idx, base, last, weights, gain, trig, state["sq"], 0, 2)
    ys.append(y)
    layout.append(tuple(x.shape[0] for x in last))
    step = 1
    while step < n:
        sq = sq + hop(sq, [(i, i ^ step) for i in range(n)])
        step *= 2
    ys.append(qkv_chunk(idx, base, last, weights, gain, trig, jnp.zeros_like(sq), 2, 3)[0])
    res = attention(
        idx,
        sq,
        segment_ids.reshape(total, 1),
        seg_row,
        ys,
        layout,
        long,
        n,
        rows,
        HEADS * HEAD,
        clips,
    )
    outs, kv = res[:n], res[n]
    parts = [outs[0]] + [None] * (n - 1)
    for o in reversed(range(1, n)):
        parts[o] = hop(outs[o], [(i, i ^ o) for i in range(n)])
    new_cache = cache_write(page_table, kv_cache, kv)
    attended = assemble(idx, parts)
    return (attended, new_cache)


def solution(mesh):
    return jax.shard_map(
        functools.partial(body, n=mesh.shape["tp"]),
        mesh=mesh,
        in_specs=(
            P(("rep", "tp"), None),
            P(None, None, "tp"),
            P(None, "rep", None),
            P(None, "tp"),
            P("rep"),
            P(None, "rep"),
            P("rep"),
            P(None, "tp", "rep", None, None),
        ),
        out_specs=(P(("rep", "tp"), None), P(None, "tp", "rep", None, None)),
        check_vma=False,
    )
```
